1024 devices in a mesh: dp: 128 (over x_hi, z, core), space: 8 (over x_lo, y).
Axes of the slice: x: 4 (x_hi: 2, x_lo: 2; x = x_hi * 2 + x_lo), y: 4, z: 32, core: 2. Of those that a mesh axis runs over, the one named last changes fastest.
Arguments:
- features: bfloat16 [128, 40, 37, 1024], P('dp', 'space'), may hold values from -6 to 6
- weights: bfloat16 [3, 9, 1024, 128], P(None, None, 'space'), may hold values from -0.0625 to 0.0625
- bias: float32 [3, 128], replicated, may hold values from -3 to 3
- grad_out: bfloat16 [128, 40, 37, 384], P('dp', 'space'), may hold values from -6 to 6
Outputs:
- activations: bfloat16 [128, 40, 37, 384], P('dp', 'space')
- input_grad: bfloat16 [128, 40, 37, 1024], P('dp', 'space')
- weight_grad: float32 [3, 9, 1024, 128], P(None, None, 'space')
- bias_grad: float32 [3, 128], replicated
The draws below stay inside these ranges and needn't reach their ends.
All inputs are finite; a program needn't handle non-finite values.
Results may differ from the reference program's by a relative error of at most 0.0049.
Values may be sent and summed in bfloat16 or wider, within the bound.
A program may use at most 64 MiB of HBM per device.

```python
import jax
import jax.numpy as jnp
from jax import lax

CIN = 1024
COUT = 128
H = 40
W = 37
B = 128


def levels(rng, dims, cuts, low, largest):
    loudness, own = 1.0, jax.random.fold_in(rng, 6)
    for axis_at, shards_of in cuts:
        steps = jnp.exp(jax.random.uniform(jax.random.fold_in(own, axis_at), (shards_of,), jnp.float32, low / len(cuts), largest / len(cuts)))
        loudness = loudness * jnp.repeat(steps, dims[axis_at] // shards_of).reshape([-1 if axis == axis_at else 1 for axis in range(len(dims))])
    return loudness


def centred(own_key, shape, deviation, reach, split=(), kind=jnp.bfloat16):
    loudness = levels(own_key, shape, split, -0.22, 0.18) if split else 1.0
    result = jax.random.normal(own_key, shape, jnp.float32) * deviation * loudness
    return jnp.minimum(jnp.maximum(result, -reach), reach).astype(kind)


def setup_inputs(seed: int = 0) -> dict:
    arg_keys = jax.random.split(jax.random.key(seed), 5)
    features = centred(arg_keys[0], (B, H, W, CIN), 1.0, 6.0, ((0, 128), (1, 8)))
    weights = centred(arg_keys[1], (3, 9, CIN, COUT), (9 * CIN) ** -0.5, 0.0625, ((2, 8),))
    bias = centred(arg_keys[2], (3, COUT), 0.5, 3.0, (), jnp.float32)
    grad_out = centred(arg_keys[3], (B, H, W, 3 * COUT), 1.0, 6.0, ((0, 128), (1, 8)))
    return dict(features=features, weights=weights, bias=bias, grad_out=grad_out)


dilations = (12, 24, 36)
offsets = tuple((row_shift, col_shift) for row_shift in (-1, 0, 1) for col_shift in (-1, 0, 1))


def valid_span(shift, length):
    return max(0, -shift), length - max(0, shift)


def reference(features, weights, bias, grad_out):
    image_count, height, columns, channels = features.shape
    outputs = weights.shape[3]
    pixels = height * columns

    def one_image(totals, inputs_now):
        picture, upstream = inputs_now
        pre_parts = []
        for branch, spacing in enumerate(dilations):
            running = jnp.zeros((height, columns, outputs), jnp.float32)
            for tap_index, (shift_y, shift_x) in enumerate(offsets):
                step_y = shift_y * spacing
                step_x = shift_x * spacing
                row_lo, row_hi = valid_span(step_y, height)
                col_lo, col_hi = valid_span(step_x, columns)
                window = picture[row_lo + step_y:row_hi + step_y, col_lo + step_x:col_hi + step_x, :]
                product = jnp.dot(window.reshape(-1, channels), weights[branch, tap_index], preferred_element_type=jnp.float32)
                running = running.at[row_lo:row_hi, col_lo:col_hi, :].add(product.reshape(row_hi - row_lo, col_hi - col_lo, outputs))
            pre_parts.append(running.reshape(pixels, outputs) + bias[branch])
        pre_act = jnp.concatenate(pre_parts, axis=1)
        squash = jax.nn.sigmoid(pre_act)
        active = (pre_act * squash).astype(jnp.bfloat16)
        slope_terms = squash * (1.0 + pre_act * (1.0 - squash))
        grad_pre = (upstream.reshape(pixels, 3 * outputs).astype(jnp.float32) * slope_terms).astype(jnp.bfloat16)
        grad_map = grad_pre.reshape(height, columns, 3 * outputs)
        grad_input = jnp.zeros((height, columns, channels), jnp.float32)
        weight_parts = []
        bias_parts = []
        for branch, spacing in enumerate(dilations):
            first_col = branch * outputs
            branch_grad = grad_map[:, :, first_col:first_col + outputs]
            bias_parts.append(jnp.sum(branch_grad.astype(jnp.float32), axis=(0, 1)))
            tap_terms = []
            for tap_index, (shift_y, shift_x) in enumerate(offsets):
                step_y = shift_y * spacing
                step_x = shift_x * spacing
                row_lo, row_hi = valid_span(step_y, height)
                col_lo, col_hi = valid_span(step_x, columns)
                window = picture[row_lo + step_y:row_hi + step_y, col_lo + step_x:col_hi + step_x, :].reshape(-1, channels)
                grad_piece = branch_grad[row_lo:row_hi, col_lo:col_hi, :].reshape(-1, outputs)
                tap_terms.append(jnp.dot(window.T, grad_piece, preferred_element_type=jnp.float32))
                back = jnp.dot(grad_piece, weights[branch, tap_index].T, preferred_element_type=jnp.float32)
                grad_input = grad_input.at[row_lo + step_y:row_hi + step_y, col_lo + step_x:col_hi + step_x, :].add(back.reshape(row_hi - row_lo, col_hi - col_lo, channels))
            weight_parts.append(jnp.stack(tap_terms))
        totals = (totals[0] + jnp.stack(weight_parts), totals[1] + jnp.stack(bias_parts))
        return totals, (active.reshape(height, columns, 3 * outputs), grad_input.astype(jnp.bfloat16))

    initial = (jnp.zeros((3, 9, channels, outputs), jnp.float32), jnp.zeros((3, outputs), jnp.float32))
    (weight_sum, bias_sum), (activations, input_grad) = lax.scan(one_image, initial, (features, grad_out))
    return activations, input_grad, weight_sum / image_count, bias_sum / image_count
```

```python
import jax
import jax.numpy as jnp
from jax import lax
from jax.experimental import pallas as pl
from jax.experimental.pallas import tpu as pltpu
from jax.sharding import PartitionSpec as P

MESH = pl.DeviceIdType.MESH
BF = jnp.bfloat16
F32 = jnp.float32

Z = 32
ROWS = 20
COLS = 37
PITCH = 48
LEFT = 40
TAPS = 28
PAD = 18


def body(
    feat, w, bias, go, act_o, ig_o, wg_o, bg_o,
    Xr, S, XV, XT, Wf, WT, Pt, RP, GOr, AC, Gr, GVp, WG, IG, IGb,
    SC, RC, SX, RX, T2, SZ1, RZ1, T3, SZ2, RZ2, AA, bsum,
    xs, xr, gos, gor, ws, wr, wl, ps, pr, gs, gr, acs, acr, igs, igr,
    cs, cr, x_s, x_r, z1s, z1r, z2s, z2r, y2s, y2r, y1s, y1r, yxs, yxr, ycs, ycr,
):
    dp = lax.axis_index("dp")
    s = lax.axis_index("space")
    c = lax.rem(dp, 2)
    z = lax.rem(dp // 2, Z)
    u = dp // (2 * Z)
    p = s // 4
    q = lax.rem(s, 4)
    za = lax.rem(z, 4)
    zb = z // 4

    def flip(v, d, n):
        out = v
        bit = 1
        while bit < n:
            if d & bit:
                out = out + bit - 2 * bit * lax.rem(v // bit, 2)
            bit *= 2
        return out

    def dev(uu=None, zz=None, cc=None, pp=None, qq=None):
        uu = u if uu is None else uu
        zz = z if zz is None else zz
        cc = c if cc is None else cc
        pp = p if pp is None else pp
        qq = q if qq is None else qq
        return (uu * (2 * Z) + zz * 2 + cc, pp * 4 + qq)

    peers = [dev(pp=flip(p, d // 4, 2), qq=flip(q, d % 4, 4)) for d in range(1, 8)]
    peers += [dev(cc=1 - c), dev(uu=1 - u), dev(uu=1 - u, pp=1 - p)]
    peers += [dev(zz=zb * 4 + flip(za, d, 4)) for d in range(1, 4)]
    peers += [dev(zz=flip(zb, d, 8) * 4 + za) for d in range(1, 8)]
    barrier = pltpu.get_barrier_semaphore()
    for peer in peers:
        pl.semaphore_signal(barrier, inc=1, device_id=peer, device_id_type=MESH)
    pl.semaphore_wait(barrier, len(peers))

    def remote(src, dst, send, recv, peer):
        return pltpu.make_async_remote_copy(
            src_ref=src, dst_ref=dst, send_sem=send, recv_sem=recv, device_id=peer, device_id_type=MESH
        )

    def arrived(ref, sem):
        pltpu.make_async_copy(ref, ref, sem).wait()

    def feature_copies(i, start):
        row = 5 * s + i
        pp = lax.rem(row, 2)
        n = row // 2
        for qq in range(4):
            away = jnp.logical_or(pp != p, qq != q)
            for h in range(2):
                src = feat.at[0, i, :, pl.ds((qq + 4 * h) * 128, 128)]
                dst = Xr.at[n, :, pl.ds(h * 128, 128)]

                @pl.when(away)
                def _():
                    copy = remote(src, dst, xs.at[i, qq, h], xr.at[n, h], dev(pp=pp, qq=qq))
                    if start:
                        copy.start()
                    else:
                        copy.wait_send()

                if start:
                    @pl.when(jnp.logical_not(away))
                    def _():
                        pltpu.make_async_copy(src, dst, xr.at[n, h]).start()

    lax.fori_loop(0, 5, lambda i, x: (feature_copies(i, True), x)[1], 0)

    def weight_copies():
        own = Wf.at[:, pl.ds(p * 128, 128), :]
        first = remote(
            w.at[pl.ds(0, 14)], Wf.at[pl.ds(0, 14), pl.ds(p * 128, 128), :], ws.at[0], wr.at[0], dev(pp=1 - p)
        )
        second = remote(
            w.at[pl.ds(14, 13)], Wf.at[pl.ds(14, 13), pl.ds(p * 128, 128), :], ws.at[1], wr.at[1],
            dev(uu=1 - u, pp=1 - p),
        )
        return first, second, pltpu.make_async_copy(w, own, wl.at[0])

    for copy in weight_copies():
        copy.start()

    def grad_copies(i, start):
        row = 5 * s + i
        pp = lax.rem(row, 2)
        qq = row // 10
        slot = lax.rem(row // 2, 5)
        away = jnp.logical_or(pp != p, qq != q)

        @pl.when(away)
        def _():
            copy = remote(go.at[0, i], GOr.at[slot], gos.at[i], gor.at[slot], dev(pp=pp, qq=qq))
            if start:
                copy.start()
            else:
                copy.wait_send()

        if start:
            @pl.when(jnp.logical_not(away))
            def _():
                pltpu.make_async_copy(go.at[0, i], GOr.at[slot], gor.at[slot]).start()

    lax.fori_loop(0, 5, lambda i, x: (grad_copies(i, True), x)[1], 0)

    def clear(n, x):
        S[n] = jnp.zeros((128, 384), F32)
        return x

    lax.fori_loop(0, ROWS, clear, 0)

    def clear_pad(n, x):
        for k in range(3):
            GVp[k, n] = jnp.zeros((PITCH, 384), BF)
            GVp[k, PAD + ROWS + n] = jnp.zeros((PITCH, 384), BF)
        return x

    lax.fori_loop(0, PAD, clear_pad, 0)
    for h in range(2):
        WG[27, h] = jnp.zeros((128, 128), F32)

    shifts = (0, -12, 12, -24, 24, -36, 36)

    def spread(n, x):
        for h in range(2):
            arrived(Xr.at[n, :, pl.ds(h * 128, 128)], xr.at[n, h])
        S[n, LEFT : LEFT + COLS, 0:256] = Xr[n].astype(F32)
        for v, d in enumerate(shifts):
            XV[v, n] = S[n, LEFT + d : LEFT + d + PITCH, 0:256].astype(BF)
        return x

    lax.fori_loop(0, ROWS, spread, 0)
    arrived(w, wl.at[0])
    arrived(Wf.at[pl.ds(0, 14), pl.ds((1 - p) * 128, 128), :], wr.at[0])
    arrived(Wf.at[pl.ds(14, 13), pl.ds((1 - p) * 128, 128), :], wr.at[1])

    def partial_copy(k, d):
        qq = flip(q, d, 4)
        return remote(
            Pt.at[k, pl.ds(5 * qq, 5)], RP.at[k, d - 1], ps.at[k, d - 1], pr.at[k, d - 1], dev(qq=qq)
        )

    def gather_copy(k, d):
        rows = Gr.at[k, pl.ds(5 * q, 5)]
        return remote(rows, rows, gs.at[k, d - 1], gr.at[k, d - 1], dev(qq=flip(q, d, 4)))

    for k in range(3):
        for a in (0, -1, 1):
            sh = 6 * (k + 1) * a
            n0, n1 = max(0, -sh), ROWS - max(0, sh)
            rows = n1 - n0
            left = jnp.concatenate(
                [XV[v, n0 + sh : n1 + sh] for v in (1 + 2 * k, 0, 2 + 2 * k)], axis=2
            ).reshape(rows * PITCH, 768)
            t = 9 * k + 3 * (a + 1)
            right = Wf[t : t + 3].reshape(768, 128)
            part = jnp.dot(left, right, preferred_element_type=F32).reshape(rows, PITCH, 128)[:, :40]
            if a == 0:
                Pt[k] = part
            else:
                Pt[k, n0:n1] += part
        for d in range(1, 4):
            partial_copy(k, d).start()

    for j in range(8):
        lo, hi = 128 * j, min(960, 128 * j + 128)
        piece = XV[0].reshape(ROWS * PITCH, 256)[lo:hi].astype(F32)
        if hi - lo < 128:
            piece = jnp.concatenate([piece, jnp.zeros((128 - (hi - lo), 256), F32)], axis=0)
        XT[:, lo : lo + 128] = jnp.transpose(piece).astype(BF)

    def turn(t, x):
        WT[t] = jnp.transpose(Wf[t].astype(F32)).astype(BF)
        return x

    lax.fori_loop(0, 27, turn, 0)
    for i in range(5):
        arrived(GOr.at[i], gor.at[i])

    for k in range(3):
        for d in range(1, 4):
            arrived(RP.at[k, d - 1], pr.at[k, d - 1])
        lanes = slice(128 * k, 128 * (k + 1))
        for i in range(5):
            pre = Pt[k, 5 * q + i] + RP[k, 0, i] + RP[k, 1, i] + RP[k, 2, i] + bias[k : k + 1, :]
            pre = pre[:COLS]
            squash = jax.nn.sigmoid(pre)
            AC[i, :, lanes] = (pre * squash).astype(BF)
            slope = squash * (1.0 + pre * (1.0 - squash))
            Gr[k, 5 * q + i] = (GOr[i, :, lanes].astype(F32) * slope).astype(BF)
        for d in range(1, 4):
            gather_copy(k, d).start()

    def act_copies(i, start):
        row = 10 * q + p + 2 * i
        owner = row // 5
        local = lax.rem(row, 5)
        away = owner != s
        dst = act_o.at[0, local]

        @pl.when(away)
        def _():
            copy = remote(AC.at[i], dst, acs.at[i], acr.at[local], (dp, owner))
            if start:
                copy.start()
            else:
                copy.wait_send()

        if start:
            @pl.when(jnp.logical_not(away))
            def _():
                pltpu.make_async_copy(AC.at[i], dst, acr.at[local]).start()

    lax.fori_loop(0, 5, lambda i, x: (act_copies(i, True), x)[1], 0)

    spans = ((0, 9), (9, 9), (18, 10))

    def core_copy(k):
        lo, size = spans[k]
        return remote(
            SC.at[pl.ds(lo, size)], RC.at[pl.ds(lo, size)], cs.at[k], cr.at[k], dev(cc=1 - c)
        )

    def cross_copy(k, d):
        lo, size = spans[k]
        h, uu = flip(p, d % 2, 2), flip(u, d // 2, 2)
        return remote(
            SX.at[h, uu, pl.ds(lo, size)], RX.at[d - 1, pl.ds(lo, size)], x_s.at[k, d - 1], x_r.at[k, d - 1],
            dev(uu=uu, pp=h),
        )

    def cross_stage(k):
        lo, size = spans[k]
        arrived(RC.at[pl.ds(lo, size)], cr.at[k])

        def add(t, x):
            for h in range(2):
                for uu in range(2):
                    here = WG[t, h, pl.ds(c * 64 + uu * 32, 32), :]
                    SX[h, uu, t] = (here + RC[t, h, uu * 32 : uu * 32 + 32].astype(F32)).astype(BF)
            T2[t] = WG[t, p, pl.ds(c * 64 + u * 32, 32), :] + RC[t, p, pl.ds(u * 32, 32), :].astype(F32)
            return x

        lax.fori_loop(lo, lo + size, add, 0)
        for d in range(1, 4):
            cross_copy(k, d).start()

    for k in range(3):
        for d in range(1, 4):
            arrived(Gr.at[k, pl.ds(5 * flip(q, d, 4), 5)], gr.at[k, d - 1])

        def widen(n, total):
            row = Gr[k, n].astype(F32)
            S[n, LEFT : LEFT + COLS, 256:384] = row
            for cc in range(3):
                d = -12 * (k + 1) * (cc - 1)
                GVp[k, PAD + n, :, 128 * cc : 128 * cc + 128] = S[n, LEFT + d : LEFT + d + PITCH, 256:384].astype(BF)
            return total + jnp.sum(row, axis=0, keepdims=True)

        bsum[k : k + 1, :] = lax.fori_loop(0, ROWS, widen, jnp.zeros((1, 128), F32))
        flat = GVp[k].reshape((ROWS + 2 * PAD) * PITCH, 384)
        for a in (-1, 0, 1):
            sh = 6 * (k + 1) * a
            n0, n1 = max(0, sh), ROWS + min(0, sh)
            f0 = (PITCH * n0) // 128 * 128
            f1 = -(-(PITCH * n1) // 128) * 128
            base = (PAD - sh) * PITCH
            res = jnp.dot(XT[:, f0:f1], flat[base + f0 : base + f1], preferred_element_type=F32)
            for cc in range(3):
                for h in range(2):
                    WG[9 * k + 3 * (a + 1) + cc, h] = res[128 * h : 128 * h + 128, 128 * cc : 128 * cc + 128]
        if k == 2:
            for h in range(2):
                WG[27, h, 0:3] = bsum[0:3]
        lo, size = spans[k]

        def stage(t, x):
            for h in range(2):
                SC[t, h] = WG[t, h, pl.ds((1 - c) * 64, 64), :].astype(BF)
            return x

        lax.fori_loop(lo, lo + size, stage, 0)
        core_copy(k).start()
        if k > 0:
            cross_stage(k - 1)
    cross_stage(2)

    for k in range(3):
        for a in (0, -1, 1):
            sh = 6 * (k + 1) * a
            n0, n1 = max(0, sh), ROWS + min(0, sh)
            rows = n1 - n0
            left = GVp[k, PAD + n0 - sh : PAD + n1 - sh].reshape(rows * PITCH, 384)
            t = 9 * k + 3 * (a + 1)
            right = WT[t : t + 3].reshape(384, 256)
            part = jnp.dot(left, right, preferred_element_type=F32).reshape(rows, PITCH, 256)
            if k == 0 and a == 0:
                IG[...] = part
            else:
                IG[n0:n1] += part

    def input_copies(n, start):
        row = 2 * n + p
        owner = row // 5
        local = lax.rem(row, 5)
        away = owner != s
        for h in range(2):
            src = IGb.at[n, :, pl.ds(h * 128, 128)]
            dst = ig_o.at[0, local, :, pl.ds((q + 4 * h) * 128, 128)]

            @pl.when(away)
            def _():
                copy = remote(src, dst, igs.at[n, h], igr.at[local, q, h], (dp, owner))
                if start:
                    copy.start()
                else:
                    copy.wait_send()

            if start:
                @pl.when(jnp.logical_not(away))
                def _():
                    pltpu.make_async_copy(src, dst, igr.at[local, q, h]).start()

    def finish(n, x):
        IGb[n] = IG[n, :COLS].astype(BF)
        input_copies(n, True)
        return x

    lax.fori_loop(0, ROWS, finish, 0)

    for k in range(3):
        for d in range(1, 4):
            lo, size = spans[k]
            arrived(RX.at[d - 1, pl.ds(lo, size)], x_r.at[k, d - 1])

    def first_copy(d):
        ta = flip(za, d, 4)
        return remote(SZ1.at[ta], RZ1.at[d - 1], z1s.at[d - 1], z1r.at[d - 1], dev(zz=zb * 4 + ta))

    def sum_x(tb, x):
        for ta in range(4):
            t = 4 * tb + ta
            T2[t] = T2[t] + RX[0, t].astype(F32) + RX[1, t].astype(F32) + RX[2, t].astype(F32)
            SZ1[ta, tb] = T2[t].astype(BF)
        return x

    lax.fori_loop(0, 7, sum_x, 0)
    for d in range(1, 4):
        first_copy(d).start()

    for d in range(1, 4):
        arrived(RZ1.at[d - 1], z1r.at[d - 1])

    def sum_z(tb, x):
        T3[tb] = T2[4 * tb + za] + RZ1[0, tb].astype(F32) + RZ1[1, tb].astype(F32) + RZ1[2, tb].astype(F32)
        SZ2[tb] = T3[tb].astype(BF)
        return x

    lax.fori_loop(0, 7, sum_z, 0)

    def second_copy(tb):
        return remote(SZ2.at[tb], RZ2.at[zb], z2s.at[tb], z2r.at[zb], dev(zz=tb * 4 + za))

    def back_copy(b):
        own = AA.at[c, u, za, zb]
        return remote(own, own, y2s.at[b], y2r.at[zb], dev(zz=b * 4 + za))

    for tb in range(7):
        @pl.when(zb != tb)
        def _():
            second_copy(tb).start()

    @pl.when(zb < 7)
    def _():
        total = T3[zb]
        for b in range(8):
            @pl.when(zb != b)
            def _():
                arrived(RZ2.at[b], z2r.at[b])
        for b in range(8):
            total = total + jnp.where(zb != b, RZ2[b].astype(F32), 0.0)
        AA[c, u, za, zb] = (total * (1.0 / 128.0)).astype(BF)
        for b in range(8):
            @pl.when(zb != b)
            def _():
                back_copy(b).start()

    for b in range(7):
        @pl.when(zb != b)
        def _():
            arrived(AA.at[c, u, za, b], y2r.at[b])

    def around_copy(d):
        mine = AA.at[c, u, za]
        return remote(mine, mine, y1s.at[d - 1], y1r.at[d - 1], dev(zz=zb * 4 + flip(za, d, 4)))

    for d in range(1, 4):
        around_copy(d).start()
    for d in range(1, 4):
        arrived(AA.at[c, u, flip(za, d, 4)], y1r.at[d - 1])
    across = remote(AA.at[c, u], AA.at[c, u], yxs.at[0], yxr.at[0], dev(uu=1 - u))
    across.start()
    arrived(AA.at[c, 1 - u], yxr.at[0])
    beside = remote(AA.at[c], AA.at[c], ycs.at[0], ycr.at[0], dev(cc=1 - c))
    beside.start()
    arrived(AA.at[1 - c], ycr.at[0])

    def write(tb, x):
        for ta in range(4):
            t = 4 * tb + ta

            @pl.when(t < 27)
            def _():
                for cc in range(2):
                    for uu in range(2):
                        wg_o[t, cc * 64 + uu * 32 : cc * 64 + uu * 32 + 32, :] = AA[cc, uu, ta, tb].astype(F32)
        return x

    lax.fori_loop(0, 7, write, 0)
    bg_o[...] = AA[0, 0, 3, 6].astype(F32)[0:3]

    lax.fori_loop(0, 5, lambda i, x: (feature_copies(i, False), x)[1], 0)
    lax.fori_loop(0, 5, lambda i, x: (grad_copies(i, False), x)[1], 0)
    lax.fori_loop(0, 5, lambda i, x: (act_copies(i, False), x)[1], 0)
    lax.fori_loop(0, ROWS, lambda n, x: (input_copies(n, False), x)[1], 0)
    first, second, _ = weight_copies()
    first.wait_send()
    second.wait_send()
    for k in range(3):
        for d in range(1, 4):
            partial_copy(k, d).wait_send()
            gather_copy(k, d).wait_send()
            cross_copy(k, d).wait_send()
        core_copy(k).wait_send()
    for d in range(1, 4):
        first_copy(d).wait_send()
        around_copy(d).wait_send()
    for tb in range(7):
        @pl.when(zb != tb)
        def _():
            second_copy(tb).wait_send()

    @pl.when(zb < 7)
    def _():
        for b in range(8):
            @pl.when(zb != b)
            def _():
                back_copy(b).wait_send()

    across.wait_send()
    beside.wait_send()
    for i in range(5):
        arrived(act_o.at[0, i], acr.at[i])
        for qq in range(4):
            for h in range(2):
                arrived(ig_o.at[0, i, :, pl.ds((qq + 4 * h) * 128, 128)], igr.at[i, qq, h])


def per_device(features, weights, bias, grad_out):
    dma = pltpu.SemaphoreType.DMA
    V = pltpu.VMEM
    anywhere = pl.BlockSpec(memory_space=pl.ANY)
    vmem = pl.BlockSpec(memory_space=pltpu.VMEM)
    scratch = [
        V((ROWS, COLS, 256), BF), V((ROWS, 128, 384), F32), V((7, ROWS, PITCH, 256), BF), V((256, 1024), BF),
        V((27, 256, 128), BF), V((27, 128, 256), BF), V((3, ROWS, 40, 128), F32), V((3, 3, 5, 40, 128), F32),
        V((5, COLS, 384), BF), V((5, COLS, 384), BF), V((3, ROWS, COLS, 128), BF),
        V((3, ROWS + 2 * PAD, PITCH, 384), BF), V((TAPS, 2, 128, 128), F32), V((ROWS, PITCH, 256), F32),
        V((ROWS, COLS, 256), BF),
        V((TAPS, 2, 64, 128), BF), V((TAPS, 2, 64, 128), BF), V((2, 2, TAPS, 32, 128), BF), V((3, TAPS, 32, 128), BF),
        V((TAPS, 32, 128), F32), V((4, 7, 32, 128), BF), V((3, 7, 32, 128), BF), V((7, 32, 128), F32),
        V((7, 32, 128), BF), V((8, 32, 128), BF), V((2, 2, 4, 7, 32, 128), BF), V((8, 128), F32),
        dma((5, 4, 2)), dma((ROWS, 2)), dma((5,)), dma((5,)), dma((2,)), dma((2,)), dma((1,)),
        dma((3, 3)), dma((3, 3)), dma((3, 3)), dma((3, 3)), dma((5,)), dma((5,)), dma((ROWS, 2)), dma((5, 4, 2)),
        dma((3,)), dma((3,)), dma((3, 3)), dma((3, 3)), dma((3,)), dma((3,)), dma((7,)), dma((8,)),
        dma((8,)), dma((8,)), dma((3,)), dma((3,)), dma((1,)), dma((1,)), dma((1,)), dma((1,)),
    ]
    act, ig, wg, bg = pl.pallas_call(
        body,
        out_shape=(
            jax.ShapeDtypeStruct((1, 5, COLS, 384), BF),
            jax.ShapeDtypeStruct((1, 5, COLS, 1024), BF),
            jax.ShapeDtypeStruct((27, 128, 128), F32),
            jax.ShapeDtypeStruct((3, 128), F32),
        ),
        in_specs=[anywhere, anywhere, vmem, anywhere],
        out_specs=(anywhere, anywhere, vmem, vmem),
        scratch_shapes=scratch,
        compiler_params=pltpu.CompilerParams(
            collective_id=0, has_side_effects=True, vmem_limit_bytes=56 << 20
        ),
        name="pyramid",
    )(features, weights.reshape(27, 128, 128), bias, grad_out)
    return act, ig, wg.reshape(3, 9, 128, 128), bg


def solution(mesh):
    placed = (
        P("dp", "space", None, None),
        P(None, None, "space", None),
        P(),
        P("dp", "space", None, None),
    )
    return jax.shard_map(
        per_device,
        mesh=mesh,
        in_specs=placed,
        out_specs=(
            P("dp", "space", None, None),
            P("dp", "space", None, None),
            P(None, None, "space", None),
            P(),
        ),
        check_vma=False,
    )
```

```python
import jax
import jax.numpy as jnp
from jax import lax
from jax.experimental import pallas as pl
from jax.experimental.pallas import tpu as pltpu
from jax.sharding import PartitionSpec as P

MESH = pl.DeviceIdType.MESH
BF = jnp.bfloat16
F32 = jnp.float32

Z = 32
ROWS = 20
COLS = 37
PITCH = 48
LEFT = 40
TAPS = 28
PAD = 18


def body(
    feat, w, bias, go, act_o, ig_o, wg_o, bg_o,
    Xr, S, XV, XT, Wf, WT, Pt, RH, RP, GOr, AC, Gr, GVp, WG, IG, IGb,
    SC, RC, SX, RX, T2, SZ1, RZ1, T3, SZ2, RZ2, AA, bsum,
    xs, xr, gos, gor, ws, wr, vs, vr, wl, hs, hr, ps, pr, gs, gr, acs, acr, igs, igr,
    cs, cr, x_s, x_r, z1s, z1r, z2s, z2r, y2s, y2r, y1s, y1r, yxs, yxr, ycs, ycr,
):
    dp = lax.axis_index("dp")
    s = lax.axis_index("space")
    c = lax.rem(dp, 2)
    z = lax.rem(dp // 2, Z)
    u = dp // (2 * Z)
    p = s // 4
    q = lax.rem(s, 4)
    za = lax.rem(z, 4)
    zb = z // 4

    def flip_add(v, d):
        return lax.rem(v + d, 4)

    def flip(v, d, n):
        out = v
        bit = 1
        while bit < n:
            if d & bit:
                out = out + bit - 2 * bit * lax.rem(v // bit, 2)
            bit *= 2
        return out

    def dev(uu=None, zz=None, cc=None, pp=None, qq=None):
        uu = u if uu is None else uu
        zz = z if zz is None else zz
        cc = c if cc is None else cc
        pp = p if pp is None else pp
        qq = q if qq is None else qq
        return (uu * (2 * Z) + zz * 2 + cc, pp * 4 + qq)

    peers = [dev(pp=flip(p, d // 4, 2), qq=flip(q, d % 4, 4)) for d in range(1, 8)]
    peers += [dev(cc=1 - c), dev(uu=1 - u), dev(uu=1 - u, pp=1 - p)]
    peers += [dev(zz=zb * 4 + flip(za, d, 4)) for d in range(1, 4)]
    peers += [dev(zz=flip(zb, d, 8) * 4 + za) for d in range(1, 8)]
    barrier = pltpu.get_barrier_semaphore()
    for peer in peers:
        pl.semaphore_signal(barrier, inc=1, device_id=peer, device_id_type=MESH)
    pl.semaphore_wait(barrier, len(peers))

    def remote(src, dst, send, recv, peer):
        return pltpu.make_async_remote_copy(
            src_ref=src, dst_ref=dst, send_sem=send, recv_sem=recv, device_id=peer, device_id_type=MESH
        )

    def arrived(ref, sem):
        pltpu.make_async_copy(ref, ref, sem).wait()

    def feature_copies(i, start):
        row = 5 * s + i
        pp = lax.rem(row, 2)
        n = row // 2
        for qq in range(4):
            away = jnp.logical_or(pp != p, qq != q)
            for h in range(2):
                src = feat.at[0, i, :, pl.ds((qq + 4 * h) * 128, 128)]
                dst = Xr.at[n, :, pl.ds(h * 128, 128)]

                @pl.when(away)
                def _():
                    copy = remote(src, dst, xs.at[i, qq, h], xr.at[n, h], dev(pp=pp, qq=qq))
                    if start:
                        copy.start()
                    else:
                        copy.wait_send()

                if start:
                    @pl.when(jnp.logical_not(away))
                    def _():
                        pltpu.make_async_copy(src, dst, xr.at[n, h]).start()

    lax.fori_loop(0, 5, lambda i, x: (feature_copies(i, True), x)[1], 0)

    pieces = ((0, 9), (9, 10), (19, 8))

    def weight_copy(j):
        lo, n = pieces[j]
        return remote(
            w.at[pl.ds(lo, n), pl.ds(c * 64, 64)], Wf.at[pl.ds(lo, n), pl.ds(p * 128 + c * 64, 64)],
            ws.at[j], wr.at[j], dev(uu=u if j == 2 else 1 - u, pp=1 - p),
        )

    def weight_part(j, cc):
        lo, n = pieces[j]
        return Wf.at[pl.ds(lo, n), pl.ds((1 - p) * 128 + cc * 64, 64)]

    def share_copy(j):
        return remote(weight_part(j, c), weight_part(j, c), vs.at[j], vr.at[j], dev(cc=1 - c))

    def share(j):
        arrived(weight_part(j, c), wr.at[j])
        share_copy(j).start()

    for j in range(3):
        weight_copy(j).start()
    pltpu.make_async_copy(w, Wf.at[:, pl.ds(p * 128, 128), :], wl.at[0]).start()

    def grad_copies(i, start):
        row = 5 * s + i
        pp = lax.rem(row, 2)
        qq = row // 10
        slot = lax.rem(row // 2, 5)
        away = jnp.logical_or(pp != p, qq != q)

        @pl.when(away)
        def _():
            copy = remote(go.at[0, i], GOr.at[slot], gos.at[i], gor.at[slot], dev(pp=pp, qq=qq))
            if start:
                copy.start()
            else:
                copy.wait_send()

        if start:
            @pl.when(jnp.logical_not(away))
            def _():
                pltpu.make_async_copy(go.at[0, i], GOr.at[slot], gor.at[slot]).start()

    lax.fori_loop(0, 5, lambda i, x: (grad_copies(i, True), x)[1], 0)

    def clear(n, x):
        S[n] = jnp.zeros((128, 384), F32)
        return x

    lax.fori_loop(0, ROWS, clear, 0)

    def clear_pad(n, x):
        for k in range(3):
            GVp[k, n] = jnp.zeros((PITCH, 384), BF)
            GVp[k, PAD + ROWS + n] = jnp.zeros((PITCH, 384), BF)
        return x

    lax.fori_loop(0, PAD, clear_pad, 0)
    for h in range(2):
        WG[27, h] = jnp.zeros((128, 128), F32)

    shifts = (0, -12, 12, -24, 24, -36, 36)

    def spread(n, x):
        for h in range(2):
            arrived(Xr.at[n, :, pl.ds(h * 128, 128)], xr.at[n, h])
        S[n, LEFT : LEFT + COLS, 0:256] = Xr[n].astype(F32)
        for v, d in enumerate(shifts):
            XV[v, n] = S[n, LEFT + d : LEFT + d + PITCH, 0:256].astype(BF)
        return x

    share(0)
    lax.fori_loop(0, ROWS, spread, 0)
    share(1)
    for j in range(8):
        lo, hi = 128 * j, min(960, 128 * j + 128)
        piece = XV[0].reshape(ROWS * PITCH, 256)[lo:hi].astype(F32)
        if hi - lo < 128:
            piece = jnp.concatenate([piece, jnp.zeros((128 - (hi - lo), 256), F32)], axis=0)
        XT[:, lo : lo + 128] = jnp.transpose(piece).astype(BF)
    share(2)
    arrived(w, wl.at[0])

    after, before, facing = flip_add(q, 1), flip_add(q, 3), flip_add(q, 2)
    halves = ((0, 3), (3, 2))

    def half_copy(k, e):
        lo, n = halves[e]
        return remote(
            Pt.at[k, pl.ds(5 * facing + lo, n)], RH.at[k, pl.ds(lo, n)], hs.at[k, e], hr.at[k, e],
            dev(qq=before if e else after),
        )

    def partial_copy(k, e):
        qq = before if e else after
        return remote(Pt.at[k, pl.ds(5 * qq, 5)], RP.at[k, e], ps.at[k, e], pr.at[k, e], dev(qq=qq))

    def pass_on(k):
        for e in range(2):
            lo, n = halves[e]
            arrived(RH.at[k, pl.ds(lo, n)], hr.at[k, e])
            first = 5 * (before if e else after) + lo
            for i in range(n):
                Pt[k, first + i] += RH[k, lo + i]
            partial_copy(k, e).start()

    def gather_copy(k, d):
        rows = Gr.at[k, pl.ds(5 * q, 5)]
        return remote(rows, rows, gs.at[k, d - 1], gr.at[k, d - 1], dev(qq=flip(q, d, 4)))

    for k in range(3):
        arrived(weight_part(k, 1 - c), vr.at[k])
        for a in (0, -1, 1):
            sh = 6 * (k + 1) * a
            n0, n1 = max(0, -sh), ROWS - max(0, sh)
            rows = n1 - n0
            left = jnp.concatenate(
                [XV[v, n0 + sh : n1 + sh] for v in (1 + 2 * k, 0, 2 + 2 * k)], axis=2
            ).reshape(rows * PITCH, 768)
            t = 9 * k + 3 * (a + 1)
            right = Wf[t : t + 3].reshape(768, 128)
            part = jnp.dot(left, right, preferred_element_type=F32).reshape(rows, PITCH, 128)[:, :COLS]
            if a == 0:
                Pt[k] = part
            else:
                Pt[k, n0:n1] += part
        for e in range(2):
            half_copy(k, e).start()
        if k > 0:
            pass_on(k - 1)
    pass_on(2)

    for i in range(5):
        arrived(GOr.at[i], gor.at[i])

    for k in range(3):
        for e in range(2):
            arrived(RP.at[k, e], pr.at[k, e])
        lanes = slice(128 * k, 128 * (k + 1))
        for i in range(5):
            pre = Pt[k, 5 * q + i] + RP[k, 0, i] + RP[k, 1, i] + bias[k : k + 1, :]
            squash = jax.nn.sigmoid(pre)
            AC[i, :, lanes] = (pre * squash).astype(BF)
            slope = squash * (1.0 + pre * (1.0 - squash))
            Gr[k, 5 * q + i] = (GOr[i, :, lanes].astype(F32) * slope).astype(BF)
        for d in range(1, 4):
            gather_copy(k, d).start()

    def act_copies(i, start):
        row = 10 * q + p + 2 * i
        owner = row // 5
        local = lax.rem(row, 5)
        away = owner != s
        dst = act_o.at[0, local]

        @pl.when(away)
        def _():
            copy = remote(AC.at[i], dst, acs.at[i], acr.at[local], (dp, owner))
            if start:
                copy.start()
            else:
                copy.wait_send()

        if start:
            @pl.when(jnp.logical_not(away))
            def _():
                pltpu.make_async_copy(AC.at[i], dst, acr.at[local]).start()

    lax.fori_loop(0, 5, lambda i, x: (act_copies(i, True), x)[1], 0)

    spans = ((0, 9), (9, 9), (18, 10))

    def core_copy(k):
        lo, size = spans[k]
        return remote(
            SC.at[pl.ds(lo, size)], RC.at[pl.ds(lo, size)], cs.at[k], cr.at[k], dev(cc=1 - c)
        )

    def cross_copy(k, d):
        lo, size = spans[k]
        h, uu = flip(p, d % 2, 2), flip(u, d // 2, 2)
        return remote(
            SX.at[h, uu, pl.ds(lo, size)], RX.at[d - 1, pl.ds(lo, size)], x_s.at[k, d - 1], x_r.at[k, d - 1],
            dev(uu=uu, pp=h),
        )

    def cross_stage(k):
        lo, size = spans[k]
        arrived(RC.at[pl.ds(lo, size)], cr.at[k])

        def add(t, x):
            for h in range(2):
                for uu in range(2):
                    here = WG[t, h, pl.ds(c * 64 + uu * 32, 32), :]
                    SX[h, uu, t] = (here + RC[t, h, uu * 32 : uu * 32 + 32].astype(F32)).astype(BF)
            T2[t] = WG[t, p, pl.ds(c * 64 + u * 32, 32), :] + RC[t, p, pl.ds(u * 32, 32), :].astype(F32)
            return x

        lax.fori_loop(lo, lo + size, add, 0)
        for d in range(1, 4):
            cross_copy(k, d).start()

    for k in range(3):
        for d in range(1, 4):
            arrived(Gr.at[k, pl.ds(5 * flip(q, d, 4), 5)], gr.at[k, d - 1])

        def widen(n, total):
            row = Gr[k, n].astype(F32)
            S[n, LEFT : LEFT + COLS, 256:384] = row
            for cc in range(3):
                d = -12 * (k + 1) * (cc - 1)
                GVp[k, PAD + n, :, 128 * cc : 128 * cc + 128] = S[n, LEFT + d : LEFT + d + PITCH, 256:384].astype(BF)
            return total + jnp.sum(row, axis=0, keepdims=True)

        bsum[k : k + 1, :] = lax.fori_loop(0, ROWS, widen, jnp.zeros((1, 128), F32))
        flat = GVp[k].reshape((ROWS + 2 * PAD) * PITCH, 384)
        for a in (-1, 0, 1):
            sh = 6 * (k + 1) * a
            n0, n1 = max(0, sh), ROWS + min(0, sh)
            f0 = (PITCH * n0) // 128 * 128
            f1 = -(-(PITCH * n1) // 128) * 128
            base = (PAD - sh) * PITCH
            res = jnp.dot(XT[:, f0:f1], flat[base + f0 : base + f1], preferred_element_type=F32)
            for cc in range(3):
                for h in range(2):
                    WG[9 * k + 3 * (a + 1) + cc, h] = res[128 * h : 128 * h + 128, 128 * cc : 128 * cc + 128]
        if k == 2:
            for h in range(2):
                WG[27, h, 0:3] = bsum[0:3]
        lo, size = spans[k]

        def stage(t, x):
            for h in range(2):
                SC[t, h] = WG[t, h, pl.ds((1 - c) * 64, 64), :].astype(BF)
            return x

        lax.fori_loop(lo, lo + size, stage, 0)
        core_copy(k).start()
        if k > 0:
            cross_stage(k - 1)
    cross_stage(2)

    def turn(t, x):
        WT[t] = jnp.transpose(Wf[t].astype(F32)).astype(BF)
        return x

    lax.fori_loop(0, 27, turn, 0)

    for k in range(3):
        for a in (0, -1, 1):
            sh = 6 * (k + 1) * a
            n0, n1 = max(0, sh), ROWS + min(0, sh)
            rows = n1 - n0
            left = GVp[k, PAD + n0 - sh : PAD + n1 - sh].reshape(rows * PITCH, 384)
            t = 9 * k + 3 * (a + 1)
            right = WT[t : t + 3].reshape(384, 256)
            part = jnp.dot(left, right, preferred_element_type=F32).reshape(rows, PITCH, 256)
            if k == 0 and a == 0:
                IG[...] = part
            else:
                IG[n0:n1] += part

    def input_copies(n, start):
        row = 2 * n + p
        owner = row // 5
        local = lax.rem(row, 5)
        away = owner != s
        for h in range(2):
            src = IGb.at[n, :, pl.ds(h * 128, 128)]
            dst = ig_o.at[0, local, :, pl.ds((q + 4 * h) * 128, 128)]

            @pl.when(away)
            def _():
                copy = remote(src, dst, igs.at[n, h], igr.at[local, q, h], (dp, owner))
                if start:
                    copy.start()
                else:
                    copy.wait_send()

            if start:
                @pl.when(jnp.logical_not(away))
                def _():
                    pltpu.make_async_copy(src, dst, igr.at[local, q, h]).start()

    def finish(n, x):
        IGb[n] = IG[n, :COLS].astype(BF)
        input_copies(n, True)
        return x

    lax.fori_loop(0, ROWS, finish, 0)

    for k in range(3):
        for d in range(1, 4):
            lo, size = spans[k]
            arrived(RX.at[d - 1, pl.ds(lo, size)], x_r.at[k, d - 1])

    def first_copy(d):
        ta = flip(za, d, 4)
        return remote(SZ1.at[ta], RZ1.at[d - 1], z1s.at[d - 1], z1r.at[d - 1], dev(zz=zb * 4 + ta))

    def sum_x(tb, x):
        for ta in range(4):
            t = 4 * tb + ta
            T2[t] = T2[t] + RX[0, t].astype(F32) + RX[1, t].astype(F32) + RX[2, t].astype(F32)
            SZ1[ta, tb] = T2[t].astype(BF)
        return x

    lax.fori_loop(0, 7, sum_x, 0)
    for d in range(1, 4):
        first_copy(d).start()

    for d in range(1, 4):
        arrived(RZ1.at[d - 1], z1r.at[d - 1])

    def sum_z(tb, x):
        T3[tb] = T2[4 * tb + za] + RZ1[0, tb].astype(F32) + RZ1[1, tb].astype(F32) + RZ1[2, tb].astype(F32)
        SZ2[tb] = T3[tb].astype(BF)
        return x

    lax.fori_loop(0, 7, sum_z, 0)

    def second_copy(tb):
        return remote(SZ2.at[tb], RZ2.at[zb], z2s.at[tb], z2r.at[zb], dev(zz=tb * 4 + za))

    def back_copy(b):
        own = AA.at[c, u, za, zb]
        return remote(own, own, y2s.at[b], y2r.at[zb], dev(zz=b * 4 + za))

    for tb in range(7):
        @pl.when(zb != tb)
        def _():
            second_copy(tb).start()

    @pl.when(zb < 7)
    def _():
        total = T3[zb]
        for b in range(8):
            @pl.when(zb != b)
            def _():
                arrived(RZ2.at[b], z2r.at[b])
        for b in range(8):
            total = total + jnp.where(zb != b, RZ2[b].astype(F32), 0.0)
        AA[c, u, za, zb] = (total * (1.0 / 128.0)).astype(BF)
        for b in range(8):
            @pl.when(zb != b)
            def _():
                back_copy(b).start()

    for b in range(7):
        @pl.when(zb != b)
        def _():
            arrived(AA.at[c, u, za, b], y2r.at[b])

    def around_copy(d):
        mine = AA.at[c, u, za]
        return remote(mine, mine, y1s.at[d - 1], y1r.at[d - 1], dev(zz=zb * 4 + flip(za, d, 4)))

    for d in range(1, 4):
        around_copy(d).start()
    for d in range(1, 4):
        arrived(AA.at[c, u, flip(za, d, 4)], y1r.at[d - 1])
    across = remote(AA.at[c, u], AA.at[c, u], yxs.at[0], yxr.at[0], dev(uu=1 - u))
    across.start()
    arrived(AA.at[c, 1 - u], yxr.at[0])
    beside = remote(AA.at[c], AA.at[c], ycs.at[0], ycr.at[0], dev(cc=1 - c))
    beside.start()
    arrived(AA.at[1 - c], ycr.at[0])

    def write(tb, x):
        for ta in range(4):
            t = 4 * tb + ta

            @pl.when(t < 27)
            def _():
                for cc in range(2):
                    for uu in range(2):
                        wg_o[t, cc * 64 + uu * 32 : cc * 64 + uu * 32 + 32, :] = AA[cc, uu, ta, tb].astype(F32)
        return x

    lax.fori_loop(0, 7, write, 0)
    bg_o[...] = AA[0, 0, 3, 6].astype(F32)[0:3]

    lax.fori_loop(0, 5, lambda i, x: (feature_copies(i, False), x)[1], 0)
    lax.fori_loop(0, 5, lambda i, x: (grad_copies(i, False), x)[1], 0)
    lax.fori_loop(0, 5, lambda i, x: (act_copies(i, False), x)[1], 0)
    lax.fori_loop(0, ROWS, lambda n, x: (input_copies(n, False), x)[1], 0)
    for j in range(3):
        weight_copy(j).wait_send()
        share_copy(j).wait_send()
    for k in range(3):
        for e in range(2):
            half_copy(k, e).wait_send()
            partial_copy(k, e).wait_send()
        for d in range(1, 4):
            gather_copy(k, d).wait_send()
            cross_copy(k, d).wait_send()
        core_copy(k).wait_send()
    for d in range(1, 4):
        first_copy(d).wait_send()
        around_copy(d).wait_send()
    for tb in range(7):
        @pl.when(zb != tb)
        def _():
            second_copy(tb).wait_send()

    @pl.when(zb < 7)
    def _():
        for b in range(8):
            @pl.when(zb != b)
            def _():
                back_copy(b).wait_send()

    across.wait_send()
    beside.wait_send()
    for i in range(5):
        arrived(act_o.at[0, i], acr.at[i])
        for qq in range(4):
            for h in range(2):
                arrived(ig_o.at[0, i, :, pl.ds((qq + 4 * h) * 128, 128)], igr.at[i, qq, h])


def per_device(features, weights, bias, grad_out):
    dma = pltpu.SemaphoreType.DMA
    V = pltpu.VMEM
    anywhere = pl.BlockSpec(memory_space=pl.ANY)
    vmem = pl.BlockSpec(memory_space=pltpu.VMEM)
    scratch = [
        V((ROWS, COLS, 256), BF), V((ROWS, 128, 384), F32), V((7, ROWS, PITCH, 256), BF), V((256, 1024), BF),
        V((27, 256, 128), BF), V((27, 128, 256), BF), V((3, ROWS, COLS, 128), F32), V((3, 5, COLS, 128), F32),
        V((3, 2, 5, COLS, 128), F32),
        V((5, COLS, 384), BF), V((5, COLS, 384), BF), V((3, ROWS, COLS, 128), BF),
        V((3, ROWS + 2 * PAD, PITCH, 384), BF), V((TAPS, 2, 128, 128), F32), V((ROWS, PITCH, 256), F32),
        V((ROWS, COLS, 256), BF),
        V((TAPS, 2, 64, 128), BF), V((TAPS, 2, 64, 128), BF), V((2, 2, TAPS, 32, 128), BF), V((3, TAPS, 32, 128), BF),
        V((TAPS, 32, 128), F32), V((4, 7, 32, 128), BF), V((3, 7, 32, 128), BF), V((7, 32, 128), F32),
        V((7, 32, 128), BF), V((8, 32, 128), BF), V((2, 2, 4, 7, 32, 128), BF), V((8, 128), F32),
        dma((5, 4, 2)), dma((ROWS, 2)), dma((5,)), dma((5,)), dma((3,)), dma((3,)), dma((3,)), dma((3,)), dma((1,)),
        dma((3, 2)), dma((3, 2)), dma((3, 2)), dma((3, 2)), dma((3, 3)), dma((3, 3)), dma((5,)), dma((5,)), dma((ROWS, 2)), dma((5, 4, 2)),
        dma((3,)), dma((3,)), dma((3, 3)), dma((3, 3)), dma((3,)), dma((3,)), dma((7,)), dma((8,)),
        dma((8,)), dma((8,)), dma((3,)), dma((3,)), dma((1,)), dma((1,)), dma((1,)), dma((1,)),
    ]
    act, ig, wg, bg = pl.pallas_call(
        body,
        out_shape=(
            jax.ShapeDtypeStruct((1, 5, COLS, 384), BF),
            jax.ShapeDtypeStruct((1, 5, COLS, 1024), BF),
            jax.ShapeDtypeStruct((27, 128, 128), F32),
            jax.ShapeDtypeStruct((3, 128), F32),
        ),
        in_specs=[anywhere, anywhere, vmem, anywhere],
        out_specs=(anywhere, anywhere, vmem, vmem),
        scratch_shapes=scratch,
        compiler_params=pltpu.CompilerParams(
            collective_id=0, has_side_effects=True, vmem_limit_bytes=56 << 20
        ),
        name="pyramid",
    )(features, weights.reshape(27, 128, 128), bias, grad_out)
    return act, ig, wg.reshape(3, 9, 128, 128), bg


def solution(mesh):
    placed = (
        P("dp", "space", None, None),
        P(None, None, "space", None),
        P(),
        P("dp", "space", None, None),
    )
    return jax.shard_map(
        per_device,
        mesh=mesh,
        in_specs=placed,
        out_specs=(
            P("dp", "space", None, None),
            P("dp", "space", None, None),
            P(None, None, "space", None),
            P(),
        ),
        check_vma=False,
    )
```
